32 devices in a mesh: row: 4 (over z), col: 8 (over y, x, core).
Axes of the slice: x: 2, y: 2, z: 4, core: 2. Of those that a mesh axis runs over, the one named last changes fastest.
Arguments:
- activations: bfloat16 [1024, 12288], P('col', 'row'), may hold values from -45 to 45
- qkv_weight: bfloat16 [12288, 3, 12288], P('row', None, 'col'), may hold values from -0.108253175 to 0.108253175
- out_weight: bfloat16 [12288, 12288], P('col', 'row'), may hold values from -0.21875 to 0.21875
Outputs:
- attn_out: bfloat16 [1024, 12288], P('col', 'row')
The draws below stay inside these ranges and needn't reach their ends.
All inputs are finite; a program needn't handle non-finite values.
Results may differ from the reference program's by a relative error of at most 0.012.
The reference program's roundings to bfloat16 on the way (of `normed`, `projected` and `attended`) count: a program that leaves them out, or rounds other values in their place, can miss the bound.
Values may be sent and summed in bfloat16 or wider, within the bound.
No kernel may reach another device: no remote copies, remote signals or barrier semaphores. Data moves between devices by JAX's collectives and lax.ppermute only.
A program may use at most 128 MiB of HBM per device.

```python
import math
import jax
import jax.numpy as jnp
from jax import lax

D = 12288
HEADS = 96
HEAD_DIM = 128
SEQ = 1024


def shared_parts(key):
    ramp = 1.0 + 2.0 * jnp.arange(D, dtype=jnp.float32) / (D - 1)
    rough = jnp.exp(jax.random.uniform(jax.random.fold_in(key, 92), (D,), jnp.float32) * math.log(10.0))
    column_scale = ramp * rough / 10.0
    return column_scale


def draw_activations(key, part):
    column_scale = shared_parts(key)
    base = jnp.clip(jax.random.normal(jax.random.fold_in(key, 14), (SEQ, D), jnp.float32), -5.0, 5.0)
    values = base * column_scale[None, :]
    return values.astype(jnp.bfloat16)


def draw_qkv_weight(key, part):
    spread = 1.0 / math.sqrt(D)
    query_weight = jnp.clip(jax.random.normal(jax.random.fold_in(key, 25), (D, D), jnp.float32), -4.0, 4.0) * spread
    key_weight = jnp.clip(jax.random.normal(jax.random.fold_in(key, 26), (D, D), jnp.float32), -4.0, 4.0) * spread
    value_weight = jnp.clip(jax.random.normal(jax.random.fold_in(key, 27), (D, D), jnp.float32), -4.0, 4.0) * spread
    return jnp.stack([query_weight, key_weight, value_weight], axis=1).astype(jnp.bfloat16)


def levels(own_key, shape, shards, smallest, largest):
    loudness = 1.0
    for axis_at, blocks in shards:
        heights = jax.random.uniform(jax.random.fold_in(jax.random.fold_in(own_key, 6), axis_at), (blocks,), jnp.float32, smallest / len(shards), largest / len(shards))
        loudness = loudness * jnp.repeat(jnp.exp(heights), shape[axis_at] // blocks).reshape((-1,) + (1,) * (len(shape) - 1 - axis_at))
    return loudness


def scatter_about(own_key, extent, deviation, bound, split=(), held_as=jnp.bfloat16):
    factor_of = levels(own_key, extent, split, -0.22, 0.18) if split else 1.0
    values = jax.random.normal(own_key, extent, jnp.float32) * deviation * factor_of
    return jnp.minimum(jnp.maximum(values, -bound), bound).astype(held_as)


def setup_inputs(seed: int = 0) -> dict:
    key_list = jax.random.split(jax.random.key(seed), 4)
    activations = draw_activations(jax.random.fold_in(key_list[3], 71), 0)
    qkv_weight = draw_qkv_weight(jax.random.fold_in(key_list[3], 71), 0)
    out_weight = scatter_about(key_list[2], (D, D), (D // 16) ** -0.5, 0.21875, ((0, 8), (1, 4)))
    return {"activations": activations, "qkv_weight": qkv_weight, "out_weight": out_weight}


epsilon = 1e-05

def layer_normed(widened, totals, squares):
    average = totals / D
    variance = squares / D - average * average
    return ((widened - average[:, None]) * lax.rsqrt(variance + epsilon)[:, None]).astype(jnp.bfloat16)

def reference(activations, qkv_weight, out_weight):
    widened = activations.astype(jnp.float32)
    totals = lax.optimization_barrier(jnp.sum(widened, 1))
    squares = lax.optimization_barrier(jnp.sum(widened * widened, 1))
    normed = layer_normed(widened, totals, squares)
    projected = jnp.dot(normed, qkv_weight.reshape(D, 3 * D), preferred_element_type=jnp.float32).astype(jnp.bfloat16)
    seq_total = activations.shape[0]
    positions = jnp.arange(seq_total, dtype=jnp.int32)
    allowed = positions[:, None] >= positions[None, :]
    score_scale = 1.0 / HEAD_DIM ** 0.5

    def one_head(head):
        offset = (head * HEAD_DIM).astype(jnp.int32)
        queries = lax.dynamic_slice_in_dim(projected, offset, HEAD_DIM, 1)
        key_part = lax.dynamic_slice_in_dim(projected, offset + D, HEAD_DIM, 1)
        value_part = lax.dynamic_slice_in_dim(projected, offset + 2 * D, HEAD_DIM, 1)
        scores = jnp.dot(queries, key_part.T, preferred_element_type=jnp.float32) * score_scale
        scores = jnp.where(allowed, scores, jnp.float32(-1e+30))
        row_max = lax.optimization_barrier(jnp.max(scores, 1))
        weights = jnp.where(allowed, jnp.exp(scores - row_max[:, None]), jnp.float32(0.0))
        denominator = lax.optimization_barrier(jnp.sum(weights, 1))
        mixed = jnp.dot(weights.astype(jnp.bfloat16), value_part, preferred_element_type=jnp.float32)
        return (mixed / denominator[:, None]).astype(jnp.bfloat16)
    per_head = lax.map(one_head, jnp.arange(HEADS, dtype=jnp.int32))
    attended = per_head.transpose(1, 0, 2).reshape(seq_total, D)
    summed = jnp.dot(attended, out_weight, preferred_element_type=jnp.float32)
    return summed.astype(jnp.bfloat16)
```

```python
from functools import partial

import jax
import jax.numpy as jnp
from jax import lax
from jax.experimental import pallas as pl
from jax.experimental.pallas import tpu as pltpu
from jax.sharding import PartitionSpec as P

D = 12288
HEAD_DIM = 128
QUERY_BLOCK = 256


epsilon = 1e-05


def layer_normed(widened, totals, squares):
    average = totals / D
    variance = squares / D - average * average
    return ((widened - average[:, None]) * lax.rsqrt(variance + epsilon)[:, None]).astype(
        jnp.bfloat16
    )


def attend_kernel(q_ref, k_ref, v_ref, out_ref):
    tokens = q_ref.shape[0]
    block = min(QUERY_BLOCK, tokens)
    score_scale = 1.0 / HEAD_DIM**0.5
    for first in range(0, tokens, block):
        last = first + block
        scores = (
            lax.dot_general(
                q_ref[first:last, :],
                k_ref[:last, :],
                (((1,), (1,)), ((), ())),
                preferred_element_type=jnp.float32,
            )
            * score_scale
        )
        query_pos = first + lax.broadcasted_iota(jnp.int32, scores.shape, 0)
        key_pos = lax.broadcasted_iota(jnp.int32, scores.shape, 1)
        scores = jnp.where(query_pos >= key_pos, scores, jnp.float32(-1e30))
        weights = jnp.exp(scores - jnp.max(scores, axis=1, keepdims=True))
        denominator = jnp.sum(weights, axis=1, keepdims=True)
        mixed = jnp.dot(
            weights.astype(jnp.bfloat16), v_ref[:last, :], preferred_element_type=jnp.float32
        )
        out_ref[first:last, :] = (mixed / denominator).astype(jnp.bfloat16)


def attend(queries, keys, values):
    return pl.pallas_call(
        attend_kernel,
        out_shape=jax.ShapeDtypeStruct(queries.shape, jnp.bfloat16),
        name="attend",
    )(queries, keys, values)


def summed_over_row(value):
    size = lax.axis_size("row")
    total = value
    for shift in range(1, size):
        total = total + lax.ppermute(
            value, "row", [(at, (at + shift) % size) for at in range(size)]
        )
    return total


def per_device(activations, qkv_weight, out_weight):
    row_size = lax.axis_size("row")
    col_size = lax.axis_size("col")
    row_at = lax.axis_index("row")
    tokens = activations.shape[0] * col_size
    width = activations.shape[1]
    head_cols = qkv_weight.shape[2]
    half_heads = head_cols // HEAD_DIM // 2
    last_row = row_size - 1
    steps = half_heads + last_row

    widened = activations.astype(jnp.float32)
    sums = summed_over_row(jnp.stack([jnp.sum(widened, 1), jnp.sum(widened * widened, 1)]))
    normed = layer_normed(widened, sums[0], sums[1])
    gathered = lax.all_gather(normed, "col", axis=0, tiled=True)
    weight = qkv_weight.transpose(1, 2, 0)
    half = tokens // 2
    streams = [gathered[:half], gathered[half:]]

    def head_weight(head):
        return lax.dynamic_slice(
            weight, (0, head * HEAD_DIM, 0), (3, HEAD_DIM, width)
        ).reshape(3 * HEAD_DIM, width)

    def partial_sum(rows, head_w):
        return lax.dot_general(
            rows, head_w, (((1,), (1,)), ((), ())), preferred_element_type=jnp.float32
        )

    up_in = [None, None]
    down_in = [None, None]
    low_parts = []
    high_parts = []
    for step in range(steps):
        up_head = half_heads + jnp.clip(step - row_at, 0, half_heads - 1)
        down_head = jnp.clip(step - (last_row - row_at), 0, half_heads - 1)
        up_weight = head_weight(up_head)
        down_weight = head_weight(down_head)
        up_pairs = [(at, at + 1) for at in range(last_row) if 0 <= step - at < half_heads]
        down_pairs = [
            (last_row - at, last_row - at - 1)
            for at in range(last_row)
            if 0 <= step - at < half_heads
        ]
        finals = []
        for stream in range(2):
            up = partial_sum(streams[stream], up_weight)
            down = partial_sum(streams[stream], down_weight)
            if up_in[stream] is not None:
                up = up + up_in[stream].astype(jnp.float32)
                down = down + down_in[stream].astype(jnp.float32)
            up = up.astype(jnp.bfloat16)
            down = down.astype(jnp.bfloat16)
            if up_pairs:
                up_in[stream] = lax.ppermute(up, "row", up_pairs)
                down_in[stream] = lax.ppermute(down, "row", down_pairs)
            if step >= last_row:
                finals.append(jnp.where(row_at == 0, down, up))
        if step >= last_row:
            projected = jnp.concatenate(finals, 0)
            attended = attend(
                projected[:, :HEAD_DIM],
                projected[:, HEAD_DIM : 2 * HEAD_DIM],
                projected[:, 2 * HEAD_DIM :],
            )
            low = attended
            high = attended
            low_sum = attended
            high_sum = attended
            for at in range(last_row):
                low = lax.ppermute(low, "row", [(at, at + 1)])
                high = lax.ppermute(high, "row", [(last_row - at, last_row - at - 1)])
                low_sum = jnp.where(row_at == at + 1, low, low_sum)
                high_sum = jnp.where(row_at == last_row - at - 1, high, high_sum)
            low_parts.append(low_sum)
            high_parts.append(high_sum)
    all_attended = jnp.concatenate(low_parts + high_parts, 1)
    mixed = jnp.dot(all_attended, out_weight, preferred_element_type=jnp.float32)
    return lax.psum_scatter(
        mixed.astype(jnp.bfloat16), "col", scatter_dimension=0, tiled=True
    )


def solution(mesh):
    in_specs = (P("col", "row"), P("row", None, "col"), P("col", "row"))
    out_specs = P("col", "row")
    return jax.shard_map(
        per_device, mesh=mesh, in_specs=in_specs, out_specs=out_specs, check_vma=False
    )
```

```python
from functools import partial

import jax
import jax.numpy as jnp
from jax import lax
from jax.experimental import pallas as pl
from jax.experimental.pallas import tpu as pltpu
from jax.sharding import PartitionSpec as P

D = 12288
HEAD_DIM = 128
QUERY_BLOCK = 256


epsilon = 1e-05


def layer_normed(widened, totals, squares):
    average = totals / D
    variance = squares / D - average * average
    return ((widened - average[:, None]) * lax.rsqrt(variance + epsilon)[:, None]).astype(
        jnp.bfloat16
    )


def attend_kernel(first_ref, second_ref, out_ref):
    tokens = out_ref.shape[0]
    half = tokens // 2
    block = min(QUERY_BLOCK, half)
    score_scale = 1.0 / HEAD_DIM**0.5
    columns = [slice(kind * HEAD_DIM, (kind + 1) * HEAD_DIM) for kind in range(3)]
    pieces = (first_ref, second_ref)

    def keys_until(kind, last):
        whole = [ref[: min(last - at * half, half), columns[kind]] for at, ref in enumerate(pieces) if last > at * half]
        return whole[0] if len(whole) == 1 else jnp.concatenate(whole, 0)

    for first in range(0, tokens, block):
        last = first + block
        ref = pieces[first // half]
        scores = (
            lax.dot_general(
                ref[first % half : first % half + block, columns[0]],
                keys_until(1, last),
                (((1,), (1,)), ((), ())),
                preferred_element_type=jnp.float32,
            )
            * score_scale
        )
        query_pos = first + lax.broadcasted_iota(jnp.int32, scores.shape, 0)
        key_pos = lax.broadcasted_iota(jnp.int32, scores.shape, 1)
        scores = jnp.where(query_pos >= key_pos, scores, jnp.float32(-1e30))
        weights = jnp.exp(scores - jnp.max(scores, axis=1, keepdims=True))
        denominator = jnp.sum(weights, axis=1, keepdims=True)
        mixed = jnp.dot(
            weights.astype(jnp.bfloat16),
            keys_until(2, last),
            preferred_element_type=jnp.float32,
        )
        out_ref[first:last, :] = (mixed / denominator).astype(jnp.bfloat16)


def near(value):
    return pltpu.with_memory_space_constraint(value, pltpu.VMEM)


IN_VMEM = pl.BlockSpec(memory_space=pltpu.VMEM)


def attend(first, second):
    tokens = 2 * first.shape[0]
    return pl.pallas_call(
        attend_kernel,
        in_specs=[IN_VMEM, IN_VMEM],
        out_specs=IN_VMEM,
        out_shape=pltpu.VMEM((tokens, HEAD_DIM), jnp.bfloat16),
        compiler_params=pltpu.CompilerParams(vmem_limit_bytes=24 * 2**20),
        cost_estimate=pl.CostEstimate(
            flops=4 * tokens * tokens * HEAD_DIM,
            transcendentals=tokens * tokens,
            bytes_accessed=8 * tokens * HEAD_DIM,
        ),
        name="attend",
    )(near(first), near(second))


def project_kernel(step, stream, has_in, has_own, where_ref, rows_ref, weight_ref, *refs):
    refs = list(refs)
    ins = [refs.pop(0) if has else None for has in has_in]
    own = refs.pop(0) if has_own else None
    outs = [refs.pop(0), refs.pop(0)]
    rows, held, arrived = refs
    half = rows.shape[0]
    rows_copy = pltpu.make_async_copy(
        rows_ref.at[stream * half : (stream + 1) * half, :], rows, arrived.at[3, 0]
    )
    rows_copy.start()
    copies = {}
    for kind in range(3):
        for flow in range(2):
            column = pl.multiple_of(where_ref[step, flow] * HEAD_DIM, HEAD_DIM)
            copies[kind, flow] = pltpu.make_async_copy(
                weight_ref.at[kind, :, pl.ds(column, HEAD_DIM)],
                held.at[kind, :, flow * HEAD_DIM : (flow + 1) * HEAD_DIM],
                arrived.at[kind, flow],
            )
            copies[kind, flow].start()
    rows_copy.wait()
    for kind in range(3):
        copies[kind, 0].wait()
        copies[kind, 1].wait()
        total = jnp.dot(rows[...], held[kind], preferred_element_type=jnp.float32)
        columns = slice(kind * HEAD_DIM, (kind + 1) * HEAD_DIM)
        for flow in range(2):
            part = total[:, flow * HEAD_DIM : (flow + 1) * HEAD_DIM]
            if has_in[1 - flow]:
                part = part + ins[1 - flow][:, columns].astype(jnp.float32)
            outs[flow][:, columns] = part.astype(jnp.bfloat16)
    if has_own:
        columns = slice(3 * HEAD_DIM, 4 * HEAD_DIM)
        for flow in range(2):
            came = ins[1 - flow]

            @pl.when(where_ref[step, 2 + flow] == 1)
            def _():
                outs[flow][:, columns] = own[stream * half : (stream + 1) * half, :]

            if came is not None and came.shape[1] > 3 * HEAD_DIM:

                @pl.when(where_ref[step, 2 + flow] == 0)
                def _():
                    outs[flow][:, columns] = came[:, columns]

            else:

                @pl.when(where_ref[step, 2 + flow] == 0)
                def _():
                    outs[flow][:, columns] = jnp.zeros((half, HEAD_DIM), jnp.bfloat16)


def project(step, stream, where, rows, weight, ins, own):
    tokens, width = rows.shape
    half = tokens // 2
    count = 3 if own is None else 4
    operands = [where, rows, weight]
    operands += [near(value) for value in ins if value is not None]
    if own is not None:
        operands.append(near(own))
    far = pl.BlockSpec(memory_space=pl.ANY)
    in_specs = [pl.BlockSpec(memory_space=pltpu.SMEM), far, far]
    in_specs += [IN_VMEM] * (len(operands) - 3)
    return pl.pallas_call(
        partial(
            project_kernel, step, stream, [value is not None for value in ins], own is not None
        ),
        in_specs=in_specs,
        out_specs=[IN_VMEM, IN_VMEM],
        out_shape=[pltpu.VMEM((half, count * HEAD_DIM), jnp.bfloat16)] * 2,
        scratch_shapes=[
            pltpu.VMEM((half, width), jnp.bfloat16),
            pltpu.VMEM((3, width, 2 * HEAD_DIM), jnp.bfloat16),
            pltpu.SemaphoreType.DMA((4, 2)),
        ],
        compiler_params=pltpu.CompilerParams(vmem_limit_bytes=24 * 2**20),
        cost_estimate=pl.CostEstimate(
            flops=12 * half * width * HEAD_DIM,
            transcendentals=0,
            bytes_accessed=12 * width * HEAD_DIM,
        ),
        name="project",
    )(*operands)


def summed_over_row(value):
    size = lax.axis_size("row")
    total = value
    for shift in range(1, size):
        total = total + lax.ppermute(
            value, "row", [(at, (at + shift) % size) for at in range(size)]
        )
    return total


def per_device(activations, qkv_weight, out_weight):
    row_size = lax.axis_size("row")
    col_size = lax.axis_size("col")
    row_at = lax.axis_index("row")
    tokens = activations.shape[0] * col_size
    width = activations.shape[1]
    head_cols = qkv_weight.shape[2]
    half_heads = head_cols // HEAD_DIM // 2
    last_row = row_size - 1
    steps = half_heads + last_row

    widened = activations.astype(jnp.float32)
    sums = summed_over_row(jnp.stack([jnp.sum(widened, 1), jnp.sum(widened * widened, 1)]))
    normed = layer_normed(widened, sums[0], sums[1])
    gathered = lax.all_gather(normed, "col", axis=0, tiled=True)
    weight = qkv_weight.transpose(1, 0, 2)
    swapped = row_at % 2
    step_at = jnp.arange(steps, dtype=jnp.int32)
    up_head = half_heads + jnp.clip(step_at - row_at, 0, half_heads - 1)
    down_head = jnp.clip(step_at - (last_row - row_at), 0, half_heads - 1)
    up_source = jnp.broadcast_to((row_at == 0).astype(jnp.int32), (steps,))
    down_source = jnp.broadcast_to((row_at == last_row).astype(jnp.int32), (steps,))
    where = jnp.stack(
        [
            jnp.where(swapped == 0, up_head, down_head),
            jnp.where(swapped == 0, down_head, up_head),
            jnp.where(swapped == 0, up_source, down_source),
            jnp.where(swapped == 0, down_source, up_source),
        ],
        1,
    )

    def live(step, hops):
        return 0 <= step - hops < half_heads or 0 <= step - row_size - hops < half_heads

    def swap(step, parity, value):
        pairs = []
        for at in range(parity, last_row, 2):
            if live(step, at):
                pairs.append((at, at + 1))
            if live(step, last_row - at - 1):
                pairs.append((at + 1, at))
        return lax.ppermute(value, "row", pairs) if pairs else None

    heads_done = []
    got = [(None, None), (None, None)]
    gathered_heads = {}
    for step in range(steps):
        own = heads_done[step - row_size] if step >= row_size else None
        sent = []
        for stream in range(2):
            values = project(step, stream, where, gathered, weight, got[stream], own)
            sent.append(values)
            got[stream] = tuple(swap(step, at, values[at]) for at in range(2))
        if own is not None:
            for at in range(2):
                pieces = [got[stream][at] for stream in range(2)]
                if pieces[0] is not None:
                    gathered_heads[step, at] = jnp.concatenate(
                        [piece[:, 3 * HEAD_DIM :] for piece in pieces], 0
                    )
        if step >= last_row:
            final = [values[1] for values in sent]
            if row_size % 2:
                final = [jnp.where(row_at == 0, second, first) for first, second in sent]
            heads_done.append(attend(*final))
    for step in range(steps, steps + last_row):
        own = heads_done[min(step - row_size, half_heads - 1)]
        for at in range(2):
            came = gathered_heads.get((step - 1, 1 - at), own)
            value = jnp.where(where[0, 2 + at] == 1, own, came)
            moved = swap(step, at, value)
            if moved is not None:
                gathered_heads[step, at] = moved
    low_parts = []
    high_parts = []
    for head in range(half_heads):
        low = heads_done[head]
        high = heads_done[head]
        for at in range(1, row_size):
            step = head + last_row + at
            low = jnp.where(row_at == at, gathered_heads[step, (at + 1) % 2], low)
            other = last_row - at
            high = jnp.where(row_at == other, gathered_heads[step, other % 2], high)
        low_parts.append(low)
        high_parts.append(high)
    all_attended = jnp.concatenate(low_parts + high_parts, 1)
    mixed = jnp.dot(all_attended, out_weight, preferred_element_type=jnp.float32)
    return lax.psum_scatter(
        mixed.astype(jnp.bfloat16), "col", scatter_dimension=0, tiled=True
    )


def solution(mesh):
    in_specs = (P("col", "row"), P("row", None, "col"), P("col", "row"))
    out_specs = P("col", "row")
    return jax.shard_map(
        per_device, mesh=mesh, in_specs=in_specs, out_specs=out_specs, check_vma=False
    )
```

```python
from functools import partial

import jax
import jax.numpy as jnp
from jax import lax
from jax.experimental import pallas as pl
from jax.experimental.pallas import tpu as pltpu
from jax.sharding import PartitionSpec as P

D = 12288
HEAD_DIM = 128
QUERY_BLOCK = 256


epsilon = 1e-05


def layer_normed(widened, totals, squares):
    average = totals / D
    variance = squares / D - average * average
    return ((widened - average[:, None]) * lax.rsqrt(variance + epsilon)[:, None]).astype(
        jnp.bfloat16
    )


def attend_kernel(first_ref, second_ref, out_ref):
    tokens = out_ref.shape[0]
    half = tokens // 2
    block = min(QUERY_BLOCK, half)
    score_scale = 1.0 / HEAD_DIM**0.5
    columns = [slice(kind * HEAD_DIM, (kind + 1) * HEAD_DIM) for kind in range(3)]
    pieces = (first_ref, second_ref)

    def keys_until(kind, last):
        whole = [ref[: min(last - at * half, half), columns[kind]] for at, ref in enumerate(pieces) if last > at * half]
        return whole[0] if len(whole) == 1 else jnp.concatenate(whole, 0)

    for first in range(0, tokens, block):
        last = first + block
        ref = pieces[first // half]
        scores = (
            lax.dot_general(
                ref[first % half : first % half + block, columns[0]],
                keys_until(1, last),
                (((1,), (1,)), ((), ())),
                preferred_element_type=jnp.float32,
            )
            * score_scale
        )
        query_pos = first + lax.broadcasted_iota(jnp.int32, scores.shape, 0)
        key_pos = lax.broadcasted_iota(jnp.int32, scores.shape, 1)
        scores = jnp.where(query_pos >= key_pos, scores, jnp.float32(-1e30))
        weights = jnp.exp(scores - jnp.max(scores, axis=1, keepdims=True))
        denominator = jnp.sum(weights, axis=1, keepdims=True)
        mixed = jnp.dot(
            weights.astype(jnp.bfloat16),
            keys_until(2, last),
            preferred_element_type=jnp.float32,
        )
        out_ref[first:last, :] = (mixed / denominator).astype(jnp.bfloat16)


def near(value):
    return pltpu.with_memory_space_constraint(value, pltpu.VMEM)


IN_VMEM = pl.BlockSpec(memory_space=pltpu.VMEM)


def attend(first, second):
    tokens = 2 * first.shape[0]
    return pl.pallas_call(
        attend_kernel,
        in_specs=[IN_VMEM, IN_VMEM],
        out_specs=IN_VMEM,
        out_shape=pltpu.VMEM((tokens, HEAD_DIM), jnp.bfloat16),
        compiler_params=limit(24),
        cost_estimate=pl.CostEstimate(
            flops=4 * tokens * tokens * HEAD_DIM,
            transcendentals=tokens * tokens,
            bytes_accessed=8 * tokens * HEAD_DIM,
        ),
        name="attend",
    )(near(first), near(second))


def weight_copies(weight_ref, held, arrived, where_ref, step):
    for kind in range(3):
        for flow in range(2):
            column = pl.multiple_of(where_ref[step, flow] * HEAD_DIM, HEAD_DIM)
            yield pltpu.make_async_copy(
                weight_ref.at[kind, :, pl.ds(column, HEAD_DIM)],
                held.at[kind, :, flow * HEAD_DIM : (flow + 1) * HEAD_DIM],
                arrived.at[kind, flow],
            )


def hold_kernel(where_ref, weight_ref, held, arrived):
    copies = list(weight_copies(weight_ref, held, arrived, where_ref, 0))
    for copy in copies:
        copy.start()
    for copy in copies:
        copy.wait()


def stage_kernel(from_ref, to_ref, arrived):
    copy = pltpu.make_async_copy(from_ref, to_ref, arrived)
    copy.start()
    copy.wait()


FAR = pl.BlockSpec(memory_space=pl.ANY)
IN_SMEM = pl.BlockSpec(memory_space=pltpu.SMEM)


def limit(mebibytes):
    return pltpu.CompilerParams(vmem_limit_bytes=mebibytes * 2**20)


def held_shape(weight):
    return pltpu.VMEM((3, weight.shape[1], 2 * HEAD_DIM), jnp.bfloat16)


def hold(where, weight):
    return pl.pallas_call(
        hold_kernel,
        in_specs=[IN_SMEM, FAR],
        out_specs=IN_VMEM,
        out_shape=held_shape(weight),
        scratch_shapes=[pltpu.SemaphoreType.DMA((3, 2))],
        compiler_params=limit(4),
        name="hold",
    )(where, weight)


def stage(value):
    return pl.pallas_call(
        stage_kernel,
        in_specs=[FAR],
        out_specs=IN_VMEM,
        out_shape=pltpu.VMEM(value.shape, value.dtype),
        scratch_shapes=[pltpu.SemaphoreType.DMA],
        compiler_params=limit(4),
        name="stage",
    )(value)


def project_kernel(step, stream, has_in, has_own, has_next, where_ref, rows_ref, held, *refs):
    refs = list(refs)
    weight_ref = refs.pop(0) if has_next else None
    ins = [refs.pop(0) if has else None for has in has_in]
    own = refs.pop(0) if has_own else None
    outs = [refs.pop(0), refs.pop(0)]
    half = rows_ref.shape[0] // 2
    copies = []
    if has_next:
        copies = list(weight_copies(weight_ref, refs[0], refs[1], where_ref, step + 1))
        for copy in copies:
            copy.start()

    def one_kind(kind, carry):
        rows = rows_ref[stream * half : (stream + 1) * half, :]
        total = jnp.dot(rows, held[kind], preferred_element_type=jnp.float32)
        columns = pl.ds(pl.multiple_of(kind * HEAD_DIM, HEAD_DIM), HEAD_DIM)
        for flow in range(2):
            part = total[:, flow * HEAD_DIM : (flow + 1) * HEAD_DIM]
            if has_in[1 - flow]:
                part = part + ins[1 - flow][:, columns].astype(jnp.float32)
            outs[flow][:, columns] = part.astype(jnp.bfloat16)
        return carry

    lax.fori_loop(0, 3, one_kind, 0)
    if has_own:
        columns = slice(3 * HEAD_DIM, 4 * HEAD_DIM)
        for flow in range(2):
            came = ins[1 - flow]

            @pl.when(where_ref[step, 2 + flow] == 1)
            def _():
                outs[flow][:, columns] = own[stream * half : (stream + 1) * half, :]

            @pl.when(where_ref[step, 2 + flow] == 0)
            def _():
                if came is not None and came.shape[1] > 3 * HEAD_DIM:
                    outs[flow][:, columns] = came[:, columns]
                else:
                    outs[flow][:, columns] = jnp.zeros((half, HEAD_DIM), jnp.bfloat16)

    for copy in copies:
        copy.wait()


def project(step, stream, where, rows, held, weight, ins, own):
    tokens, width = rows.shape
    half = tokens // 2
    count = 3 if own is None else 4
    operands = [where, near(rows), near(held)]
    in_specs = [IN_SMEM, IN_VMEM, IN_VMEM]
    if weight is not None:
        operands.append(weight)
        in_specs.append(FAR)
    more = [near(value) for value in (*ins, own) if value is not None]
    operands += more
    in_specs += [IN_VMEM] * len(more)
    out_shape = [pltpu.VMEM((half, count * HEAD_DIM), jnp.bfloat16)] * 2
    scratch = []
    if weight is not None:
        out_shape.append(held_shape(weight))
        scratch.append(pltpu.SemaphoreType.DMA((3, 2)))
    return pl.pallas_call(
        partial(
            project_kernel,
            step,
            stream,
            [value is not None for value in ins],
            own is not None,
            weight is not None,
        ),
        in_specs=in_specs,
        out_specs=[IN_VMEM] * len(out_shape),
        out_shape=out_shape,
        scratch_shapes=scratch,
        compiler_params=limit(16),
        cost_estimate=pl.CostEstimate(
            flops=12 * half * width * HEAD_DIM,
            transcendentals=0,
            bytes_accessed=12 * width * HEAD_DIM,
        ),
        name="project",
    )(*operands)


def assemble_kernel(plan, block, place_ref, *refs):
    out_ref = refs[-1]
    for column, choices in enumerate(plan):
        to = slice(column * HEAD_DIM, (column + 1) * HEAD_DIM)
        for row_at, pieces in enumerate(choices):

            @pl.when(place_ref[0] == row_at)
            def _():
                at = 1
                for ref in (refs[index] for index in pieces):
                    cols = ref.shape[1]
                    for first in range(0, ref.shape[0], block):
                        row = pl.multiple_of(place_ref[at] * block, block)
                        out_ref[pl.ds(row, block), to] = ref[
                            first : first + block, cols - HEAD_DIM :
                        ]
                        at += 1


def assemble(place, tokens, block, wanted):
    operands = []
    plan = []
    for choices in wanted:
        numbered = []
        for pieces in choices:
            numbers = []
            for piece in pieces:
                known = [at for at, value in enumerate(operands) if value is piece]
                if not known:
                    operands.append(piece)
                    known = [len(operands) - 1]
                numbers.append(known[0])
            numbered.append(numbers)
        plan.append(numbered)
    return pl.pallas_call(
        partial(assemble_kernel, plan, block),
        in_specs=[IN_SMEM] + [IN_VMEM] * len(operands),
        out_specs=IN_VMEM,
        out_shape=pltpu.VMEM((tokens, len(wanted) * HEAD_DIM), jnp.bfloat16),
        compiler_params=limit(8),
        name="assemble",
    )(place, *(near(value) for value in operands))


MIX_COLS = 256


def mix_kernel(parts, first_col, orders, block, has_base, rows_ref, weight_ref, *refs):
    refs = list(refs)
    base = refs.pop(0) if has_base else None
    *outs, held, arrived = refs
    cols = held.shape[1]
    step_cols = min(MIX_COLS, cols)

    def copies(at):
        done = 0
        start = pl.multiple_of(at * step_cols, step_cols)
        for number, (first, count) in enumerate(parts):
            yield pltpu.make_async_copy(
                weight_ref.at[pl.ds(first, count), pl.ds(first_col + start, step_cols)],
                held.at[pl.ds(done, count), pl.ds(start, step_cols)],
                arrived.at[at, number],
            )
            done += count

    for at in range(cols // step_cols):
        for copy in copies(at):
            copy.start()

    def one_step(at, carry):
        for copy in copies(at):
            copy.wait()
        columns = pl.ds(pl.multiple_of(at * step_cols, step_cols), step_cols)
        total = jnp.dot(rows_ref[...], held[:, columns], preferred_element_type=jnp.float32)
        if has_base:
            total = total + base[:, columns]
        if orders is None:
            outs[0][:, columns] = total
        else:
            for out, order in zip(outs, orders):
                for to, position in enumerate(order):
                    out[to * block : (to + 1) * block, columns] = total[
                        position * block : (position + 1) * block, :
                    ].astype(out.dtype)
        return carry

    lax.fori_loop(0, cols // step_cols, one_step, 0)


def mix(rows, weight, parts, first_col, cols, base, orders, block):
    tokens = rows.shape[0]
    operands = [near(rows), weight]
    if base is not None:
        operands.append(near(base))
    if orders is None:
        out_shape = [pltpu.VMEM((tokens, cols), jnp.float32)]
    else:
        out_shape = [
            pltpu.VMEM((tokens // 2, cols), jnp.float32),
            pltpu.VMEM((tokens // 2, cols), jnp.bfloat16),
        ]
    out = pl.pallas_call(
        partial(mix_kernel, parts, first_col, orders, block, base is not None),
        in_specs=[IN_VMEM, FAR] + [IN_VMEM] * (len(operands) - 2),
        out_specs=[IN_VMEM] * len(out_shape),
        out_shape=out_shape,
        scratch_shapes=[
            pltpu.VMEM((rows.shape[1], cols), jnp.bfloat16),
            pltpu.SemaphoreType.DMA((cols // min(MIX_COLS, cols), len(parts))),
        ],
        compiler_params=limit(16),
        cost_estimate=pl.CostEstimate(
            flops=2 * tokens * rows.shape[1] * cols,
            transcendentals=0,
            bytes_accessed=2 * rows.shape[1] * cols,
        ),
        name="mix",
    )(*operands)
    return out[0] if orders is None else out


def split_orders(bits):
    positions = [0]
    for bit in reversed(bits[1:]):
        positions = positions + [position | 1 << bit for position in positions]
    return positions, [position | 1 << bits[0] for position in positions]


def summed_over_row(value):
    size = lax.axis_size("row")
    total = value
    for shift in range(1, size):
        total = total + lax.ppermute(
            value, "row", [(at, (at + shift) % size) for at in range(size)]
        )
    return total


def per_device(activations, qkv_weight, out_weight):
    row_size = lax.axis_size("row")
    col_size = lax.axis_size("col")
    row_at = lax.axis_index("row")
    tokens = activations.shape[0] * col_size
    width = activations.shape[1]
    head_cols = qkv_weight.shape[2]
    half_heads = head_cols // HEAD_DIM // 2
    last_row = row_size - 1
    steps = half_heads + last_row

    widened = activations.astype(jnp.float32)
    sums = summed_over_row(jnp.stack([jnp.sum(widened, 1), jnp.sum(widened * widened, 1)]))
    normed = layer_normed(widened, sums[0], sums[1])
    gathered = lax.all_gather(normed, "col", axis=0, tiled=True)
    weight = qkv_weight.transpose(1, 0, 2)
    swapped = row_at % 2
    step_at = jnp.arange(steps, dtype=jnp.int32)
    up_head = half_heads + jnp.clip(step_at - row_at, 0, half_heads - 1)
    down_head = jnp.clip(step_at - (last_row - row_at), 0, half_heads - 1)
    up_source = jnp.broadcast_to((row_at == 0).astype(jnp.int32), (steps,))
    down_source = jnp.broadcast_to((row_at == last_row).astype(jnp.int32), (steps,))
    where = jnp.stack(
        [
            jnp.where(swapped == 0, up_head, down_head),
            jnp.where(swapped == 0, down_head, up_head),
            jnp.where(swapped == 0, up_source, down_source),
            jnp.where(swapped == 0, down_source, up_source),
        ],
        1,
    )

    def live(step, hops):
        return 0 <= step - hops < half_heads or 0 <= step - row_size - hops < half_heads

    def swap(step, parity, value):
        pairs = []
        for at in range(parity, last_row, 2):
            if live(step, at):
                pairs.append((at, at + 1))
            if live(step, last_row - at - 1):
                pairs.append((at + 1, at))
        return lax.ppermute(value, "row", pairs) if pairs else None

    heads_done = []
    got = [(None, None), (None, None)]
    moved = {}
    held = hold(where, weight)
    rows = stage(gathered)
    for step in range(steps):
        own = heads_done[step - row_size] if step >= row_size else None
        sent = []
        for stream in range(2):
            ahead = weight if stream == 1 and step + 1 < steps else None
            first, second, *following = project(
                step, stream, where, rows, held, ahead, got[stream], own
            )
            sent.append((first, second))
            got[stream] = (swap(step, 0, first), swap(step, 1, second))
        if following:
            held = following[0]
        for at in range(2):
            moved[step, at] = [got[0][at], got[1][at]]
        if step >= last_row:
            final = [values[1] for values in sent]
            if row_size % 2:
                final = [jnp.where(row_at == 0, second, first) for first, second in sent]
            heads_done.append(attend(*final))
    for step in range(steps, steps + last_row):
        own = heads_done[min(step - row_size, half_heads - 1)]
        for at in range(2):
            came = moved.get((step - 1, 1 - at), [None])
            value = own
            if came[0] is not None:
                came = [piece[:, -HEAD_DIM:] for piece in came]
                came = came[0] if len(came) == 1 else jnp.concatenate(came, 0)
                value = jnp.where(where[0, 2 + at] == 1, own, came)
            received = swap(step, at, value)
            if received is not None:
                moved[step, at] = [received]

    block = tokens // col_size
    col_at = lax.axis_index("col")
    place = jnp.concatenate(
        [row_at.reshape(1), col_at ^ jnp.arange(col_size, dtype=col_at.dtype)]
    ).astype(jnp.int32)

    def sources(heads):
        low = []
        high = []
        for head in heads:
            low_choice = [[heads_done[head]]] + [None] * last_row
            high_choice = [None] * last_row + [[heads_done[head]]]
            for at in range(1, row_size):
                step = head + last_row + at
                low_choice[at] = moved[step, (at + 1) % 2]
                other = last_row - at
                high_choice[other] = moved[step, other % 2]
            low.append(low_choice)
            high.append(high_choice)
        return assemble(place, tokens, block, low + high)

    out_cols = out_weight.shape[1]
    early = max(half_heads - 2, 1)
    bits = list(range(col_size.bit_length() - 1))
    bit_orders = [bits, bits[:1] + bits[:0:-1]]

    def weight_rows(first, last):
        count = (last - first) * HEAD_DIM
        return [(first * HEAD_DIM, count), ((half_heads + first) * HEAD_DIM, count)]

    early_rows = sources(range(early))
    bases = [
        mix(
            early_rows, out_weight, weight_rows(0, early), part * out_cols // 2, out_cols // 2,
            None, None, block,
        )
        for part in range(2)
    ]
    late_rows = sources(range(early, half_heads))
    halves = []
    for part in range(2):
        keep, send = mix(
            late_rows, out_weight, weight_rows(early, half_heads), part * out_cols // 2,
            out_cols // 2, bases[part], split_orders(bit_orders[part]), block,
        )
        for number, bit in enumerate(bit_orders[part]):
            partners = [(at, at ^ 1 << bit) for at in range(col_size)]
            received = lax.ppermute(send, "col", partners).astype(jnp.float32)
            total = keep + received
            kept_rows = total.shape[0] // 2 if number + 1 < len(bits) else total.shape[0]
            keep = total[:kept_rows]
            send = total[kept_rows:].astype(jnp.bfloat16)
        halves.append(keep.astype(jnp.bfloat16))
    return jnp.concatenate(halves, 1)


def solution(mesh):
    in_specs = (P("col", "row"), P("row", None, "col"), P("col", "row"))
    out_specs = P("col", "row")
    return jax.shard_map(
        per_device, mesh=mesh, in_specs=in_specs, out_specs=out_specs, check_vma=False
    )
```

```python
from functools import partial

import jax
import jax.numpy as jnp
from jax import lax
from jax.experimental import pallas as pl
from jax.experimental.pallas import tpu as pltpu
from jax.sharding import PartitionSpec as P

D = 12288
HEAD_DIM = 128
QUERY_BLOCK = 256


epsilon = 1e-05


def layer_normed(widened, totals, squares):
    average = totals / D
    variance = squares / D - average * average
    return ((widened - average[:, None]) * lax.rsqrt(variance + epsilon)[:, None]).astype(
        jnp.bfloat16
    )


def attend_kernel(first_ref, second_ref, out_ref):
    tokens = out_ref.shape[0]
    half = tokens // 2
    block = min(QUERY_BLOCK, half)
    score_scale = 1.0 / HEAD_DIM**0.5
    columns = [slice(kind * HEAD_DIM, (kind + 1) * HEAD_DIM) for kind in range(3)]
    pieces = (first_ref, second_ref)

    def keys_until(kind, last):
        whole = [ref[: min(last - at * half, half), columns[kind]] for at, ref in enumerate(pieces) if last > at * half]
        return whole[0] if len(whole) == 1 else jnp.concatenate(whole, 0)

    for first in range(0, tokens, block):
        last = first + block
        ref = pieces[first // half]
        scores = (
            lax.dot_general(
                ref[first % half : first % half + block, columns[0]],
                keys_until(1, last),
                (((1,), (1,)), ((), ())),
                preferred_element_type=jnp.float32,
            )
            * score_scale
        )
        query_pos = first + lax.broadcasted_iota(jnp.int32, scores.shape, 0)
        key_pos = lax.broadcasted_iota(jnp.int32, scores.shape, 1)
        scores = jnp.where(query_pos >= key_pos, scores, jnp.float32(-1e30))
        weights = jnp.exp(scores - jnp.max(scores, axis=1, keepdims=True))
        denominator = jnp.sum(weights, axis=1, keepdims=True)
        mixed = jnp.dot(
            weights.astype(jnp.bfloat16),
            keys_until(2, last),
            preferred_element_type=jnp.float32,
        )
        out_ref[first:last, :] = (mixed / denominator).astype(jnp.bfloat16)


def near(value):
    return pltpu.with_memory_space_constraint(value, pltpu.VMEM)


def far(value):
    return pltpu.with_memory_space_constraint(value, pltpu.HBM)


IN_VMEM = pl.BlockSpec(memory_space=pltpu.VMEM)


def attend(first, second):
    tokens = 2 * first.shape[0]
    return pl.pallas_call(
        attend_kernel,
        in_specs=[IN_VMEM, IN_VMEM],
        out_specs=IN_VMEM,
        out_shape=pltpu.VMEM((tokens, HEAD_DIM), jnp.bfloat16),
        compiler_params=limit(24),
        cost_estimate=pl.CostEstimate(
            flops=4 * tokens * tokens * HEAD_DIM,
            transcendentals=tokens * tokens,
            bytes_accessed=8 * tokens * HEAD_DIM,
        ),
        name="attend",
    )(near(first), near(second))


def weight_copies(weight_ref, held, arrived, where_ref, step):
    for kind in range(3):
        for flow in range(2):
            column = pl.multiple_of(where_ref[step, flow] * HEAD_DIM, HEAD_DIM)
            yield pltpu.make_async_copy(
                weight_ref.at[kind, :, pl.ds(column, HEAD_DIM)],
                held.at[kind, :, flow * HEAD_DIM : (flow + 1) * HEAD_DIM],
                arrived.at[kind, flow],
            )


def hold_kernel(where_ref, weight_ref, held, arrived):
    copies = list(weight_copies(weight_ref, held, arrived, where_ref, 0))
    for copy in copies:
        copy.start()
    for copy in copies:
        copy.wait()


def stage_kernel(from_ref, to_ref, arrived):
    copy = pltpu.make_async_copy(from_ref, to_ref, arrived)
    copy.start()
    copy.wait()


FAR = pl.BlockSpec(memory_space=pl.ANY)
IN_SMEM = pl.BlockSpec(memory_space=pltpu.SMEM)


def limit(mebibytes):
    return pltpu.CompilerParams(vmem_limit_bytes=mebibytes * 2**20)


def held_shape(weight):
    return pltpu.VMEM((3, weight.shape[1], 2 * HEAD_DIM), jnp.bfloat16)


def hold(where, weight):
    return pl.pallas_call(
        hold_kernel,
        in_specs=[IN_SMEM, FAR],
        out_specs=IN_VMEM,
        out_shape=held_shape(weight),
        scratch_shapes=[pltpu.SemaphoreType.DMA((3, 2))],
        compiler_params=limit(4),
        name="hold",
    )(where, far(weight))


def stage(value):
    return pl.pallas_call(
        stage_kernel,
        in_specs=[FAR],
        out_specs=IN_VMEM,
        out_shape=pltpu.VMEM(value.shape, value.dtype),
        scratch_shapes=[pltpu.SemaphoreType.DMA],
        compiler_params=limit(4),
        name="stage",
    )(far(value))


def project_kernel(step, stream, has_in, has_own, has_next, where_ref, rows_ref, held, *refs):
    refs = list(refs)
    weight_ref = refs.pop(0) if has_next else None
    ins = [refs.pop(0) if has else None for has in has_in]
    own = refs.pop(0) if has_own else None
    outs = [refs.pop(0), refs.pop(0)]
    half = rows_ref.shape[0] // 2
    copies = []
    if has_next:
        copies = list(weight_copies(weight_ref, refs[0], refs[1], where_ref, step + 1))
        for copy in copies:
            copy.start()

    def one_kind(kind, carry):
        rows = rows_ref[stream * half : (stream + 1) * half, :]
        total = jnp.dot(rows, held[kind], preferred_element_type=jnp.float32)
        columns = pl.ds(pl.multiple_of(kind * HEAD_DIM, HEAD_DIM), HEAD_DIM)
        for flow in range(2):
            part = total[:, flow * HEAD_DIM : (flow + 1) * HEAD_DIM]
            if has_in[1 - flow]:
                part = part + ins[1 - flow][:, columns].astype(jnp.float32)
            outs[flow][:, columns] = part.astype(jnp.bfloat16)
        return carry

    lax.fori_loop(0, 3, one_kind, 0)
    if has_own:
        columns = slice(3 * HEAD_DIM, 4 * HEAD_DIM)
        for flow in range(2):
            came = ins[1 - flow]

            @pl.when(where_ref[step, 2 + flow] == 1)
            def _():
                outs[flow][:, columns] = own[stream * half : (stream + 1) * half, :]

            @pl.when(where_ref[step, 2 + flow] == 0)
            def _():
                if came is not None and came.shape[1] > 3 * HEAD_DIM:
                    outs[flow][:, columns] = came[:, columns]
                else:
                    outs[flow][:, columns] = jnp.zeros((half, HEAD_DIM), jnp.bfloat16)

    for copy in copies:
        copy.wait()


def project(step, stream, where, rows, held, weight, ins, own):
    tokens, width = rows.shape
    half = tokens // 2
    count = 3 if own is None else 4
    operands = [where, near(rows), near(held)]
    in_specs = [IN_SMEM, IN_VMEM, IN_VMEM]
    if weight is not None:
        operands.append(far(weight))
        in_specs.append(FAR)
    more = [near(value) for value in (*ins, own) if value is not None]
    operands += more
    in_specs += [IN_VMEM] * len(more)
    out_shape = [pltpu.VMEM((half, count * HEAD_DIM), jnp.bfloat16)] * 2
    scratch = []
    if weight is not None:
        out_shape.append(held_shape(weight))
        scratch.append(pltpu.SemaphoreType.DMA((3, 2)))
    return pl.pallas_call(
        partial(
            project_kernel,
            step,
            stream,
            [value is not None for value in ins],
            own is not None,
            weight is not None,
        ),
        in_specs=in_specs,
        out_specs=[IN_VMEM] * len(out_shape),
        out_shape=out_shape,
        scratch_shapes=scratch,
        compiler_params=limit(16),
        cost_estimate=pl.CostEstimate(
            flops=12 * half * width * HEAD_DIM,
            transcendentals=0,
            bytes_accessed=12 * width * HEAD_DIM,
        ),
        name="project",
    )(*operands)


def assemble_kernel(plan, block, place_ref, *refs):
    *ins, out_ref, arrived = refs

    def copies(column, pieces):
        to = slice(column * HEAD_DIM, (column + 1) * HEAD_DIM)
        at = 0
        for ref in (ins[index] for index in pieces):
            cols = ref.shape[1]
            for first in range(0, ref.shape[0], block):
                row = pl.multiple_of(place_ref[1 + at] * block, block)
                yield pltpu.make_async_copy(
                    ref.at[first : first + block, cols - HEAD_DIM : cols],
                    out_ref.at[pl.ds(row, block), to],
                    arrived.at[column, at],
                )
                at += 1

    for start in (True, False):
        for column, choices in enumerate(plan):
            for row_at, pieces in enumerate(choices):

                @pl.when(place_ref[0] == row_at)
                def _():
                    for copy in copies(column, pieces):
                        copy.start() if start else copy.wait()


def assemble(place, tokens, block, wanted, hold_in, after):
    operands = list(after)
    plan = []
    for choices in wanted:
        numbered = []
        for pieces in choices:
            numbers = []
            for piece in pieces:
                known = [at for at, value in enumerate(operands) if value is piece]
                if not known:
                    operands.append(piece)
                    known = [len(operands) - 1]
                numbers.append(known[0])
            numbered.append(numbers)
        plan.append(numbered)
    return pl.pallas_call(
        partial(assemble_kernel, plan, block),
        in_specs=[IN_SMEM] + [FAR] * len(operands),
        out_specs=IN_VMEM,
        out_shape=pltpu.VMEM((tokens, len(wanted) * HEAD_DIM), jnp.bfloat16),
        scratch_shapes=[pltpu.SemaphoreType.DMA((len(wanted), tokens // block))],
        compiler_params=limit(4),
        name="assemble",
    )(place, *(near(value) for value in after), *(hold_in(value) for value in operands[len(after) :]))


def relay_kernel(flag, where_ref, own, *refs):
    *pieces, out_ref = refs

    @pl.when(where_ref[0, flag] == 1)
    def _():
        out_ref[...] = own[...]

    @pl.when(where_ref[0, flag] == 0)
    def _():
        first = 0
        for piece in pieces:
            count, cols = piece.shape
            out_ref[first : first + count, :] = piece[:, cols - HEAD_DIM :]
            first += count


def relay(flag, where, own, pieces):
    operands = [near(own)] + [near(piece) for piece in pieces]
    return pl.pallas_call(
        partial(relay_kernel, flag),
        in_specs=[IN_SMEM] + [IN_VMEM] * len(operands),
        out_specs=IN_VMEM,
        out_shape=pltpu.VMEM(own.shape, own.dtype),
        compiler_params=limit(4),
        name="relay",
    )(where, *operands)


MIX_COLS = 256


def mix_kernel(parts, first_col, orders, block, has_base, rows_ref, weight_ref, *refs):
    refs = list(refs)
    base = refs.pop(0) if has_base else None
    *outs, held, arrived = refs
    cols = held.shape[1]
    step_cols = min(MIX_COLS, cols)

    def copies(at):
        done = 0
        start = pl.multiple_of(at * step_cols, step_cols)
        for number, (first, count) in enumerate(parts):
            yield pltpu.make_async_copy(
                weight_ref.at[pl.ds(first, count), pl.ds(first_col + start, step_cols)],
                held.at[pl.ds(done, count), pl.ds(start, step_cols)],
                arrived.at[at, number],
            )
            done += count

    for at in range(cols // step_cols):
        for copy in copies(at):
            copy.start()

    def one_step(at, carry):
        for copy in copies(at):
            copy.wait()
        columns = pl.ds(pl.multiple_of(at * step_cols, step_cols), step_cols)
        total = jnp.dot(rows_ref[...], held[:, columns], preferred_element_type=jnp.float32)
        if has_base:
            total = total + base[:, columns]
        if orders is None:
            outs[0][:, columns] = total
        else:
            for out, order in zip(outs, orders):
                for to, position in enumerate(order):
                    out[to * block : (to + 1) * block, columns] = total[
                        position * block : (position + 1) * block, :
                    ].astype(out.dtype)
        return carry

    lax.fori_loop(0, cols // step_cols, one_step, 0)


def mix(rows, weight, parts, first_col, cols, base, orders, block):
    tokens = rows.shape[0]
    operands = [near(rows), far(weight)]
    if base is not None:
        operands.append(near(base))
    if orders is None:
        out_shape = [pltpu.VMEM((tokens, cols), jnp.float32)]
    else:
        out_shape = [
            pltpu.VMEM((tokens // 2, cols), jnp.float32),
            pltpu.VMEM((tokens // 2, cols), jnp.bfloat16),
        ]
    out = pl.pallas_call(
        partial(mix_kernel, parts, first_col, orders, block, base is not None),
        in_specs=[IN_VMEM, FAR] + [IN_VMEM] * (len(operands) - 2),
        out_specs=[IN_VMEM] * len(out_shape),
        out_shape=out_shape,
        scratch_shapes=[
            pltpu.VMEM((rows.shape[1], cols), jnp.bfloat16),
            pltpu.SemaphoreType.DMA((cols // min(MIX_COLS, cols), len(parts))),
        ],
        compiler_params=limit(16),
        cost_estimate=pl.CostEstimate(
            flops=2 * tokens * rows.shape[1] * cols,
            transcendentals=0,
            bytes_accessed=2 * rows.shape[1] * cols,
        ),
        name="mix",
    )(*operands)
    return out[0] if orders is None else out


def split_orders(bits):
    positions = [0]
    for bit in reversed(bits[1:]):
        positions = positions + [position | 1 << bit for position in positions]
    return positions, [position | 1 << bits[0] for position in positions]


def summed_over_row(value):
    size = lax.axis_size("row")
    total = value
    for shift in range(1, size):
        total = total + lax.ppermute(
            value, "row", [(at, (at + shift) % size) for at in range(size)]
        )
    return total


def per_device(activations, qkv_weight, out_weight):
    row_size = lax.axis_size("row")
    col_size = lax.axis_size("col")
    row_at = lax.axis_index("row")
    tokens = activations.shape[0] * col_size
    width = activations.shape[1]
    head_cols = qkv_weight.shape[2]
    half_heads = head_cols // HEAD_DIM // 2
    last_row = row_size - 1
    steps = half_heads + last_row

    widened = activations.astype(jnp.float32)
    sums = summed_over_row(jnp.stack([jnp.sum(widened, 1), jnp.sum(widened * widened, 1)]))
    normed = layer_normed(widened, sums[0], sums[1])
    gathered = lax.all_gather(normed, "col", axis=0, tiled=True)
    weight = qkv_weight.transpose(1, 0, 2)
    swapped = row_at % 2
    step_at = jnp.arange(steps, dtype=jnp.int32)
    up_head = half_heads + jnp.clip(step_at - row_at, 0, half_heads - 1)
    down_head = jnp.clip(step_at - (last_row - row_at), 0, half_heads - 1)
    up_source = jnp.broadcast_to((row_at == 0).astype(jnp.int32), (steps,))
    down_source = jnp.broadcast_to((row_at == last_row).astype(jnp.int32), (steps,))
    where = jnp.stack(
        [
            jnp.where(swapped == 0, up_head, down_head),
            jnp.where(swapped == 0, down_head, up_head),
            jnp.where(swapped == 0, up_source, down_source),
            jnp.where(swapped == 0, down_source, up_source),
        ],
        1,
    )

    def live(step, hops):
        return 0 <= step - hops < half_heads or 0 <= step - row_size - hops < half_heads

    def swap(step, parity, value):
        pairs = []
        for at in range(parity, last_row, 2):
            if live(step, at):
                pairs.append((at, at + 1))
            if live(step, last_row - at - 1):
                pairs.append((at + 1, at))
        return lax.ppermute(value, "row", pairs) if pairs else None

    heads_done = []
    got = [(None, None), (None, None)]
    moved = {}
    held = hold(where, weight)
    rows = stage(gathered)

    def relayed(step):
        own = heads_done[min(step - row_size, half_heads - 1)]
        for at in range(2):
            came = moved.get((step - 1, 1 - at), [None])
            value = own if came[0] is None else relay(2 + at, where, own, came)
            received = swap(step, at, value)
            if received is not None:
                moved[step, at] = [received]

    for step in range(steps):
        final_step = step + 1 == steps
        if final_step:
            relayed(step)
        own = heads_done[step - row_size] if step >= row_size and not final_step else None
        sent = []
        for stream in range(2):
            ahead = weight if stream == 1 and step + 1 < steps else None
            first, second, *following = project(
                step, stream, where, rows, held, ahead, got[stream], own
            )
            sent.append((first, second))
            if not final_step:
                got[stream] = (swap(step, 0, first), swap(step, 1, second))
        if following:
            held = following[0]
        if not final_step:
            for at in range(2):
                moved[step, at] = [got[0][at], got[1][at]]
        if step >= last_row:
            final = [values[1] for values in sent]
            if row_size % 2:
                final = [jnp.where(row_at == 0, second, first) for first, second in sent]
            heads_done.append(attend(*final))
    for step in range(steps, steps + last_row):
        relayed(step)

    block = tokens // col_size
    col_at = lax.axis_index("col")
    place = jnp.concatenate(
        [row_at.reshape(1), col_at ^ jnp.arange(col_size, dtype=col_at.dtype)]
    ).astype(jnp.int32)

    def sources(heads, hold_in, after):
        low = []
        high = []
        for head in heads:
            low_choice = [[heads_done[head]]] + [None] * last_row
            high_choice = [None] * last_row + [[heads_done[head]]]
            for at in range(1, row_size):
                step = head + last_row + at
                low_choice[at] = moved[step, (at + 1) % 2]
                other = last_row - at
                high_choice[other] = moved[step, other % 2]
            low.append(low_choice)
            high.append(high_choice)
        return assemble(place, tokens, block, low + high, hold_in, after)

    out_cols = out_weight.shape[1]
    early = max(half_heads - 2, 1)
    bits = list(range(col_size.bit_length() - 1))
    bit_orders = [bits, bits[:1] + bits[:0:-1]]

    def weight_rows(first, last):
        count = (last - first) * HEAD_DIM
        return [(first * HEAD_DIM, count), ((half_heads + first) * HEAD_DIM, count)]

    early_rows = sources(range(early), far, [])
    bases = [
        mix(
            early_rows, out_weight, weight_rows(0, early), part * out_cols // 2, out_cols // 2,
            None, None, block,
        )
        for part in range(2)
    ]
    late_rows = sources(range(early, half_heads), near, bases)
    halves = []
    for part in range(2):
        keep, send = mix(
            late_rows, out_weight, weight_rows(early, half_heads), part * out_cols // 2,
            out_cols // 2, bases[part], split_orders(bit_orders[part]), block,
        )
        for number, bit in enumerate(bit_orders[part]):
            partners = [(at, at ^ 1 << bit) for at in range(col_size)]
            received = lax.ppermute(send, "col", partners).astype(jnp.float32)
            total = keep + received
            kept_rows = total.shape[0] // 2 if number + 1 < len(bits) else total.shape[0]
            keep = total[:kept_rows]
            send = total[kept_rows:].astype(jnp.bfloat16)
        halves.append(keep.astype(jnp.bfloat16))
    return jnp.concatenate(halves, 1)


def solution(mesh):
    in_specs = (P("col", "row"), P("row", None, "col"), P("col", "row"))
    out_specs = P("col", "row")
    return jax.shard_map(
        per_device, mesh=mesh, in_specs=in_specs, out_specs=out_specs, check_vma=False
    )
```

```python
from functools import partial

import jax
import jax.numpy as jnp
from jax import lax
from jax.experimental import pallas as pl
from jax.experimental.pallas import tpu as pltpu
from jax.sharding import PartitionSpec as P

D = 12288
HEAD_DIM = 128
QUERY_BLOCK = 256


epsilon = 1e-05


def attend_kernel(row_block, order_ref, first_ref, second_ref, out_ref, q_ref, k_ref, v_ref):
    tokens = out_ref.shape[0]
    half = tokens // 2
    block = min(QUERY_BLOCK, tokens)
    score_scale = 1.0 / HEAD_DIM**0.5

    def natural(position):
        return pl.ds(pl.multiple_of(order_ref[position] * row_block, row_block), row_block)

    for position in range(tokens // row_block):
        start = position * row_block
        ref = first_ref if start < half else second_ref
        start = start % half
        for kind, to in enumerate((q_ref, k_ref, v_ref)):
            to[natural(position), :] = ref[
                start : start + row_block, kind * HEAD_DIM : (kind + 1) * HEAD_DIM
            ]
    for first in range(0, tokens, block):
        last = first + block
        scores = (
            lax.dot_general(
                q_ref[first:last, :],
                k_ref[:last, :],
                (((1,), (1,)), ((), ())),
                preferred_element_type=jnp.float32,
            )
            * score_scale
        )
        query_pos = first + lax.broadcasted_iota(jnp.int32, scores.shape, 0)
        key_pos = lax.broadcasted_iota(jnp.int32, scores.shape, 1)
        scores = jnp.where(query_pos >= key_pos, scores, jnp.float32(-1e30))
        weights = jnp.exp(scores - jnp.max(scores, axis=1, keepdims=True))
        denominator = jnp.sum(weights, axis=1, keepdims=True)
        mixed = jnp.dot(
            weights.astype(jnp.bfloat16), v_ref[:last, :], preferred_element_type=jnp.float32
        )
        attended = (mixed / denominator).astype(jnp.bfloat16)
        for at in range(0, block, row_block):
            out_ref[natural((first + at) // row_block), :] = attended[at : at + row_block, :]


def near(value):
    return pltpu.with_memory_space_constraint(value, pltpu.VMEM)


def far(value):
    return pltpu.with_memory_space_constraint(value, pltpu.HBM)


IN_VMEM = pl.BlockSpec(memory_space=pltpu.VMEM)
FAR = pl.BlockSpec(memory_space=pl.ANY)
IN_SMEM = pl.BlockSpec(memory_space=pltpu.SMEM)


def attend(order, row_block, first, second):
    tokens = 2 * first.shape[0]
    return pl.pallas_call(
        partial(attend_kernel, row_block),
        in_specs=[IN_SMEM, IN_VMEM, IN_VMEM],
        out_specs=IN_VMEM,
        out_shape=pltpu.VMEM((tokens, HEAD_DIM), jnp.bfloat16),
        scratch_shapes=[pltpu.VMEM((tokens, HEAD_DIM), jnp.bfloat16)] * 3,
        compiler_params=limit(24),
        cost_estimate=pl.CostEstimate(
            flops=4 * tokens * tokens * HEAD_DIM,
            transcendentals=tokens * tokens,
            bytes_accessed=8 * tokens * HEAD_DIM,
        ),
        name="attend",
    )(order, near(first), near(second))


def weight_copies(weight_ref, held, arrived, where_ref, step):
    for kind in range(3):
        for flow in range(2):
            column = pl.multiple_of(where_ref[step, flow] * HEAD_DIM, HEAD_DIM)
            yield pltpu.make_async_copy(
                weight_ref.at[kind, :, pl.ds(column, HEAD_DIM)],
                held.at[kind, :, flow * HEAD_DIM : (flow + 1) * HEAD_DIM],
                arrived.at[kind, flow],
            )


def hold_kernel(where_ref, weight_ref, held, arrived):
    copies = list(weight_copies(weight_ref, held, arrived, where_ref, 0))
    for copy in copies:
        copy.start()
    for copy in copies:
        copy.wait()


def normalise_kernel(average_ref, scale_ref, *refs):
    *pieces, out_ref = refs
    width = out_ref.shape[1]
    row = 0
    for group in pieces:
        count, cols = group[0].shape
        rows = slice(row, row + count)
        average = average_ref[rows, :]
        scale = scale_ref[rows, :]
        start = 0
        for piece in group:
            cols = piece.shape[1]

            def one(at, carry, piece=piece, start=start):
                here = pl.ds(pl.multiple_of(at * HEAD_DIM, HEAD_DIM), HEAD_DIM)
                there = pl.ds(pl.multiple_of(start + at * HEAD_DIM, HEAD_DIM), HEAD_DIM)
                value = piece[:, here].astype(jnp.float32)
                out_ref[rows, there] = ((value - average) * scale).astype(jnp.bfloat16)
                return carry

            lax.fori_loop(0, cols // HEAD_DIM, one, 0)
            start += cols
        row += count


def normalise(average, scale, groups):
    counts = [len(group) for group in groups]

    def body(average_ref, scale_ref, *refs):
        *flat, out_ref = refs
        nested = []
        for count in counts:
            nested.append(flat[:count])
            flat = flat[count:]
        normalise_kernel(average_ref, scale_ref, *nested, out_ref)

    flat = [piece for group in groups for piece in group]
    tokens = sum(group[0].shape[0] for group in groups)
    width = sum(piece.shape[1] for piece in groups[0])
    return pl.pallas_call(
        body,
        in_specs=[IN_VMEM] * (2 + len(flat)),
        out_specs=IN_VMEM,
        out_shape=pltpu.VMEM((tokens, width), jnp.bfloat16),
        compiler_params=limit(8),
        name="normalise",
    )(near(average), near(scale), *(near(piece) for piece in flat))


def limit(mebibytes):
    return pltpu.CompilerParams(vmem_limit_bytes=mebibytes * 2**20)


def held_shape(weight):
    return pltpu.VMEM((3, weight.shape[1], 2 * HEAD_DIM), jnp.bfloat16)


def hold(where, weight):
    return pl.pallas_call(
        hold_kernel,
        in_specs=[IN_SMEM, FAR],
        out_specs=IN_VMEM,
        out_shape=held_shape(weight),
        scratch_shapes=[pltpu.SemaphoreType.DMA((3, 2))],
        compiler_params=limit(4),
        name="hold",
    )(where, far(weight))


def project_kernel(step, stream, has_in, has_own, has_next, where_ref, rows_ref, held, *refs):
    refs = list(refs)
    weight_ref = refs.pop(0) if has_next else None
    ins = [refs.pop(0) if has else None for has in has_in]
    own = refs.pop(0) if has_own else None
    outs = [refs.pop(0), refs.pop(0)]
    half = rows_ref.shape[0]
    copies = []
    if has_next:
        copies = list(weight_copies(weight_ref, refs[0], refs[1], where_ref, step + 1))
        for copy in copies:
            copy.start()

    def one_kind(kind, carry):
        total = jnp.dot(rows_ref[...], held[kind], preferred_element_type=jnp.float32)
        columns = pl.ds(pl.multiple_of(kind * HEAD_DIM, HEAD_DIM), HEAD_DIM)
        for flow in range(2):
            part = total[:, flow * HEAD_DIM : (flow + 1) * HEAD_DIM]
            if has_in[1 - flow]:
                part = part + ins[1 - flow][:, columns].astype(jnp.float32)
            outs[flow][:, columns] = part.astype(jnp.bfloat16)
        return carry

    lax.fori_loop(0, 3, one_kind, 0)
    if has_own:
        columns = slice(3 * HEAD_DIM, 4 * HEAD_DIM)
        for flow in range(2):
            came = ins[1 - flow]

            @pl.when(where_ref[step, 2 + flow] == 1)
            def _():
                outs[flow][:, columns] = own[stream * half : (stream + 1) * half, :]

            @pl.when(where_ref[step, 2 + flow] == 0)
            def _():
                if came is not None and came.shape[1] > 3 * HEAD_DIM:
                    outs[flow][:, columns] = came[:, columns]
                else:
                    outs[flow][:, columns] = jnp.zeros((half, HEAD_DIM), jnp.bfloat16)

    for copy in copies:
        copy.wait()


def project(step, stream, where, rows, held, weight, ins, own):
    half, width = rows.shape
    count = 3 if own is None else 4
    operands = [where, near(rows), near(held)]
    in_specs = [IN_SMEM, IN_VMEM, IN_VMEM]
    if weight is not None:
        operands.append(far(weight))
        in_specs.append(FAR)
    more = [near(value) for value in (*ins, own) if value is not None]
    operands += more
    in_specs += [IN_VMEM] * len(more)
    out_shape = [pltpu.VMEM((half, count * HEAD_DIM), jnp.bfloat16)] * 2
    scratch = []
    if weight is not None:
        out_shape.append(held_shape(weight))
        scratch.append(pltpu.SemaphoreType.DMA((3, 2)))
    return pl.pallas_call(
        partial(
            project_kernel,
            step,
            stream,
            [value is not None for value in ins],
            own is not None,
            weight is not None,
        ),
        in_specs=in_specs,
        out_specs=[IN_VMEM] * len(out_shape),
        out_shape=out_shape,
        scratch_shapes=scratch,
        compiler_params=limit(16),
        cost_estimate=pl.CostEstimate(
            flops=12 * half * width * HEAD_DIM,
            transcendentals=0,
            bytes_accessed=12 * width * HEAD_DIM,
        ),
        name="project",
    )(*operands)


def assemble_kernel(plan, place_ref, *refs):
    *ins, out_ref, arrived = refs

    def copies(column, pieces):
        to = slice(column * HEAD_DIM, (column + 1) * HEAD_DIM)
        row = 0
        for at, ref in enumerate(ins[index] for index in pieces):
            count, cols = ref.shape
            yield pltpu.make_async_copy(
                ref.at[:, cols - HEAD_DIM : cols],
                out_ref.at[row : row + count, to],
                arrived.at[column, at],
            )
            row += count

    for start in (True, False):
        for column, choices in enumerate(plan):
            for row_at, pieces in enumerate(choices):

                @pl.when(place_ref[0] == row_at)
                def _():
                    for copy in copies(column, pieces):
                        copy.start() if start else copy.wait()


def assemble(place, tokens, wanted, hold_in, after):
    operands = list(after)
    plan = []
    for choices in wanted:
        numbered = []
        for pieces in choices:
            numbers = []
            for piece in pieces:
                known = [at for at, value in enumerate(operands) if value is piece]
                if not known:
                    operands.append(piece)
                    known = [len(operands) - 1]
                numbers.append(known[0])
            numbered.append(numbers)
        plan.append(numbered)
    return pl.pallas_call(
        partial(assemble_kernel, plan),
        in_specs=[IN_SMEM] + [FAR] * len(operands),
        out_specs=IN_VMEM,
        out_shape=pltpu.VMEM((tokens, len(wanted) * HEAD_DIM), jnp.bfloat16),
        scratch_shapes=[pltpu.SemaphoreType.DMA((len(wanted), 2))],
        compiler_params=limit(4),
        name="assemble",
    )(place, *(near(value) for value in after), *(hold_in(value) for value in operands[len(after) :]))


def relay_kernel(flag, where_ref, own, *refs):
    *pieces, out_ref = refs

    @pl.when(where_ref[0, flag] == 1)
    def _():
        out_ref[...] = own[...]

    @pl.when(where_ref[0, flag] == 0)
    def _():
        first = 0
        for piece in pieces:
            count, cols = piece.shape
            out_ref[first : first + count, :] = piece[:, cols - HEAD_DIM :]
            first += count


def relay(flag, where, own, pieces):
    operands = [near(own)] + [near(piece) for piece in pieces]
    return pl.pallas_call(
        partial(relay_kernel, flag),
        in_specs=[IN_SMEM] + [IN_VMEM] * len(operands),
        out_specs=IN_VMEM,
        out_shape=pltpu.VMEM(own.shape, own.dtype),
        compiler_params=limit(4),
        name="relay",
    )(where, *operands)


MIX_COLS = 256


def mix_kernel(parts, first_col, orders, block, has_base, rows_ref, weight_ref, *refs):
    refs = list(refs)
    base = refs.pop(0) if has_base else None
    *outs, held, arrived = refs
    cols = held.shape[1]
    step_cols = min(MIX_COLS, cols)

    def copies(at):
        done = 0
        start = pl.multiple_of(at * step_cols, step_cols)
        for number, (first, count) in enumerate(parts):
            yield pltpu.make_async_copy(
                weight_ref.at[pl.ds(first, count), pl.ds(first_col + start, step_cols)],
                held.at[pl.ds(done, count), pl.ds(start, step_cols)],
                arrived.at[at, number],
            )
            done += count

    for at in range(cols // step_cols):
        for copy in copies(at):
            copy.start()

    def one_step(at, carry):
        for copy in copies(at):
            copy.wait()
        columns = pl.ds(pl.multiple_of(at * step_cols, step_cols), step_cols)
        total = jnp.dot(rows_ref[...], held[:, columns], preferred_element_type=jnp.float32)
        if has_base:
            total = total + base[:, columns]
        if orders is None:
            outs[0][:, columns] = total
        else:
            for out, order in zip(outs, orders):
                for to, position in enumerate(order):
                    out[to * block : (to + 1) * block, columns] = total[
                        position * block : (position + 1) * block, :
                    ].astype(out.dtype)
        return carry

    lax.fori_loop(0, cols // step_cols, one_step, 0)


def mix(rows, weight, parts, first_col, cols, base, orders, block):
    tokens = rows.shape[0]
    operands = [near(rows), far(weight)]
    if base is not None:
        operands.append(near(base))
    if orders is None:
        out_shape = [pltpu.VMEM((tokens, cols), jnp.float32)]
    else:
        out_shape = [
            pltpu.VMEM((tokens // 2, cols), jnp.float32),
            pltpu.VMEM((tokens // 2, cols), jnp.bfloat16),
        ]
    out = pl.pallas_call(
        partial(mix_kernel, parts, first_col, orders, block, base is not None),
        in_specs=[IN_VMEM, FAR] + [IN_VMEM] * (len(operands) - 2),
        out_specs=[IN_VMEM] * len(out_shape),
        out_shape=out_shape,
        scratch_shapes=[
            pltpu.VMEM((rows.shape[1], cols), jnp.bfloat16),
            pltpu.SemaphoreType.DMA((cols // min(MIX_COLS, cols), len(parts))),
        ],
        compiler_params=limit(16),
        cost_estimate=pl.CostEstimate(
            flops=2 * tokens * rows.shape[1] * cols,
            transcendentals=0,
            bytes_accessed=2 * rows.shape[1] * cols,
        ),
        name="mix",
    )(*operands)
    return out[0] if orders is None else out


def split_orders(bits):
    positions = [0]
    for bit in reversed(bits[1:]):
        positions = positions + [position | 1 << bit for position in positions]
    return positions, [position | 1 << bits[0] for position in positions]


def summed_over_row(value):
    size = lax.axis_size("row")
    total = value
    for shift in range(1, size):
        total = total + lax.ppermute(
            value, "row", [(at, (at + shift) % size) for at in range(size)]
        )
    return total


def per_device(activations, qkv_weight, out_weight):
    row_size = lax.axis_size("row")
    col_size = lax.axis_size("col")
    row_at = lax.axis_index("row")
    tokens = activations.shape[0] * col_size
    width = activations.shape[1]
    head_cols = qkv_weight.shape[2]
    half_heads = head_cols // HEAD_DIM // 2
    last_row = row_size - 1
    steps = half_heads + last_row

    bits = list(range(col_size.bit_length() - 1))
    block = activations.shape[0]
    col_at = lax.axis_index("col")
    place = row_at.reshape(1).astype(jnp.int32)
    order = (col_at ^ jnp.arange(col_size, dtype=col_at.dtype)).astype(jnp.int32)

    def across(bit, value):
        return lax.ppermute(value, "col", [(at, at ^ 1 << bit) for at in range(col_size)])

    middle = width // 2
    shards = {0: [activations[:, :middle], activations[:, middle:]]}
    whole = {0: activations}
    for position in range(2, col_size, 2):
        set_bits = [bit for bit in bits[1:] if position >> bit & 1]
        low_bit, high_bit = set_bits[0], set_bits[-1]
        if low_bit == high_bit:
            whole[position] = across(low_bit, activations)
            shards[position] = [whole[position][:, :middle], whole[position][:, middle:]]
        else:
            shards[position] = [
                across(high_bit, shards[position ^ 1 << high_bit][0]),
                across(low_bit, shards[position ^ 1 << low_bit][1]),
            ]
    groups = []
    for position in range(0, col_size, 2):
        mine = [whole[position]] if position in whole else shards[position]
        groups += [mine, [across(0, piece) for piece in mine]]

    widened = activations.astype(jnp.float32)
    sums = summed_over_row(jnp.stack([jnp.sum(widened, 1), jnp.sum(widened * widened, 1)]))
    for bit in bits:
        sums = jnp.concatenate([sums, across(bit, sums)], 1)
    average = sums[0] / D
    variance = sums[1] / D - average * average
    spread = (tokens, HEAD_DIM)
    average = jnp.broadcast_to(average[:, None], spread)
    scale = jnp.broadcast_to(lax.rsqrt(variance + epsilon)[:, None], spread)
    half = tokens // 2
    rows = [
        normalise(average[:half], scale[:half], groups[: col_size // 2]),
        normalise(average[half:], scale[half:], groups[col_size // 2 :]),
    ]
    weight = qkv_weight.transpose(1, 0, 2)
    swapped = row_at % 2
    step_at = jnp.arange(steps, dtype=jnp.int32)
    up_head = half_heads + jnp.clip(step_at - row_at, 0, half_heads - 1)
    down_head = jnp.clip(step_at - (last_row - row_at), 0, half_heads - 1)
    up_source = jnp.broadcast_to((row_at == 0).astype(jnp.int32), (steps,))
    down_source = jnp.broadcast_to((row_at == last_row).astype(jnp.int32), (steps,))
    where = jnp.stack(
        [
            jnp.where(swapped == 0, up_head, down_head),
            jnp.where(swapped == 0, down_head, up_head),
            jnp.where(swapped == 0, up_source, down_source),
            jnp.where(swapped == 0, down_source, up_source),
        ],
        1,
    )

    def live(step, hops):
        return 0 <= step - hops < half_heads or 0 <= step - row_size - hops < half_heads

    def swap(step, parity, value):
        pairs = []
        for at in range(parity, last_row, 2):
            if live(step, at):
                pairs.append((at, at + 1))
            if live(step, last_row - at - 1):
                pairs.append((at + 1, at))
        return lax.ppermute(value, "row", pairs) if pairs else None

    heads_done = []
    got = [(None, None), (None, None)]
    moved = {}
    held = hold(where, weight)

    def relayed(step):
        own = heads_done[min(step - row_size, half_heads - 1)]
        for at in range(2):
            came = moved.get((step - 1, 1 - at), [None])
            value = own if came[0] is None else relay(2 + at, where, own, came)
            received = swap(step, at, value)
            if received is not None:
                moved[step, at] = [received]

    for step in range(steps):
        final_step = step + 1 == steps
        if final_step:
            relayed(step)
        own = heads_done[step - row_size] if step >= row_size and not final_step else None
        sent = []
        for stream in range(2):
            ahead = weight if stream == 1 and step + 1 < steps else None
            first, second, *following = project(
                step, stream, where, rows[stream], held, ahead, got[stream], own
            )
            sent.append((first, second))
            if not final_step:
                got[stream] = (swap(step, 0, first), swap(step, 1, second))
        if following:
            held = following[0]
        if not final_step:
            for at in range(2):
                moved[step, at] = [got[0][at], got[1][at]]
        if step >= last_row:
            final = [values[1] for values in sent]
            if row_size % 2:
                final = [jnp.where(row_at == 0, second, first) for first, second in sent]
            heads_done.append(attend(order, block, *final))
    for step in range(steps, steps + last_row):
        relayed(step)

    def sources(heads, hold_in, after):
        low = []
        high = []
        for head in heads:
            low_choice = [[heads_done[head]]] + [None] * last_row
            high_choice = [None] * last_row + [[heads_done[head]]]
            for at in range(1, row_size):
                step = head + last_row + at
                low_choice[at] = moved[step, (at + 1) % 2]
                other = last_row - at
                high_choice[other] = moved[step, other % 2]
            low.append(low_choice)
            high.append(high_choice)
        return assemble(place, tokens, low + high, hold_in, after)

    out_cols = out_weight.shape[1]
    early = max(half_heads - 2, 1)
    bit_orders = [bits, bits[:1] + bits[:0:-1]]

    def weight_rows(first, last):
        count = (last - first) * HEAD_DIM
        return [(first * HEAD_DIM, count), ((half_heads + first) * HEAD_DIM, count)]

    early_rows = sources(range(early), far, [])
    bases = [
        mix(
            early_rows, out_weight, weight_rows(0, early), part * out_cols // 2, out_cols // 2,
            None, None, block,
        )
        for part in range(2)
    ]
    late_rows = sources(range(early, half_heads), near, bases)
    halves = []
    for part in range(2):
        keep, send = mix(
            late_rows, out_weight, weight_rows(early, half_heads), part * out_cols // 2,
            out_cols // 2, bases[part], split_orders(bit_orders[part]), block,
        )
        for number, bit in enumerate(bit_orders[part]):
            partners = [(at, at ^ 1 << bit) for at in range(col_size)]
            received = lax.ppermute(send, "col", partners).astype(jnp.float32)
            total = keep + received
            kept_rows = total.shape[0] // 2 if number + 1 < len(bits) else total.shape[0]
            keep = total[:kept_rows]
            send = total[kept_rows:].astype(jnp.bfloat16)
        halves.append(keep.astype(jnp.bfloat16))
    return jnp.concatenate(halves, 1)


def solution(mesh):
    in_specs = (P("col", "row"), P("row", None, "col"), P("col", "row"))
    out_specs = P("col", "row")
    return jax.shard_map(
        per_device, mesh=mesh, in_specs=in_specs, out_specs=out_specs, check_vma=False
    )
```
